32 devices in a mesh: tensor: 4 (over x, core), section: 2 (over y), dp: 4 (over z).
Axes of the slice: x: 2, y: 2, z: 4, core: 2. Of those that a mesh axis runs over, the one named last changes fastest.
Arguments:
- block_input: bfloat16 [4096, 6144], P(('section', 'dp')), may hold values from -6 to 6
- output_gradient: bfloat16 [4096, 6144], P(('section', 'dp')), may hold values from -6 to 6
- queries: bfloat16 [4096, 3072], P(('section', 'dp'), 'tensor'), may hold values from -8 to 8
- saved_keys: bfloat16 [4096, 3072], P(('section', 'dp'), 'tensor'), may hold values from -8 to 8
- values: bfloat16 [4096, 3072], P(('section', 'dp'), 'tensor'), may hold values from -6 to 6
- document_index: int32 [4096], P(('section', 'dp')), may hold values from 0 to 4095, as said below
- output_weight: bfloat16 [6144, 3072], P(('section', 'dp'), 'tensor'), may hold values from -0.109375 to 0.109375
- adapter_down_weight: bfloat16 [2, 6144, 128], P('section'), may hold values from -0.078125 to 0.078125
- adapter_up_weight: bfloat16 [2, 128, 3072], P('section', None, 'tensor'), may hold values from -0.5 to 0.5
Outputs:
- grad_out: float32 [6144, 3072], P(('section', 'dp'), 'tensor')
- grad_value_proj: float32 [6144, 3072], P(('section', 'dp'), 'tensor')
- grad_query: bfloat16 [4096, 3072], P(('section', 'dp'), 'tensor')
- grad_key: bfloat16 [4096, 3072], P(('section', 'dp'), 'tensor')
- grad_down: float32 [2, 6144, 128], P('section', 'dp')
- grad_up: float32 [2, 128, 3072], P('section', 'dp', 'tensor')
The draws below stay inside these ranges and needn't reach their ends.
Inputs may be any that keep to these rules, and one draw needn't show every extreme that they name: `document_index`: ids never fall along the tokens; a document's id is the index of its first token, each block of 512 tokens starts a new document, and the last token is a document of its own.
All inputs are finite; a program needn't handle non-finite values.
Results may differ from the reference program's by a relative error of at most 0.015.
Values may be sent and summed in bfloat16 or wider, within the bound.
A program may use at most 192 MiB of HBM per device.

```python
import jax
import jax.numpy as jnp
from jax import lax

MODEL_WIDTH = 6144
HEADS = 24
HD = 128
ADAPTER_RANK = 128
DOC_SPAN = 128
REPLICA_TOKENS = 512
HEAD_COLUMNS = 3072
TOKENS = 4096
N_SECTION = 2
N_DP = 4


def doc_table(key):
    sub_key = jax.random.fold_in(key, 101)
    starts = jax.random.randint(sub_key, (TOKENS,), 0, DOC_SPAN) == 0
    position = jnp.arange(TOKENS, dtype=jnp.int32)
    starts = starts | (position % REPLICA_TOKENS == 0) | (position == TOKENS - 1)
    marked = jnp.where(starts, position, jnp.zeros_like(position))
    return lax.cummax(marked, axis=0)


def draw_document_index(key, part):
    return doc_table(key)


def draw_queries(key, part):
    base_key = jax.random.fold_in(key, 303)
    base = jnp.clip(jax.random.normal(base_key, (TOKENS, HEADS, HD), jnp.float32), -6.0, 6.0)
    return base.reshape(TOKENS, HEADS * HD).astype(jnp.bfloat16)


def draw_saved_keys(key, part):
    base_key = jax.random.fold_in(key, 404)
    base = jnp.clip(jax.random.normal(base_key, (TOKENS, HEADS, HD), jnp.float32), -6.0, 6.0)
    return base.reshape(TOKENS, HEADS * HD).astype(jnp.bfloat16)


def with_spikes(values, rng, source, target, blocks, factor):
    owner, partner = [(jnp.arange(values.shape[dim]) // (values.shape[dim] // blocks)).reshape([-1 if axis == dim else 1 for axis in range(values.ndim)]) for dim in (source, target)]
    chosen = jax.random.permutation(rng, blocks)[partner]
    strong = (owner == chosen) | (owner == (partner + blocks // 2) % blocks)
    return jnp.where(strong, factor * values, values)


def level_of(stream_key, shape, pieces, least, largest):
    factor_of = 1.0
    for dim, shards_of in pieces:
        steps = jax.random.uniform(jax.random.fold_in(jax.random.fold_in(stream_key, 6), dim), (shards_of,), jnp.float32, least / len(pieces), largest / len(pieces))
        factor_of = factor_of * jnp.repeat(jnp.exp(steps), shape[dim] // shards_of).reshape((-1,) + (1,) * (len(shape) - 1 - dim))
    return factor_of


def scatter_about(stream_key, extent, scale, most, pieces=(), held_as=jnp.bfloat16):
    entries = scale * jax.random.normal(stream_key, extent, jnp.float32)
    if pieces:
        entries = entries * level_of(stream_key, extent, pieces, -0.22, 0.18)
    return jnp.clip(entries, -most, most).astype(held_as)


def noise_with(stream_key, shape, spread, limit, pieces, heavy, held_as=jnp.bfloat16):
    entries = spread * jax.random.normal(stream_key, shape, jnp.float32)
    if pieces:
        entries = entries * level_of(stream_key, shape, pieces, -0.22, 0.18)
    return jnp.clip(with_spikes(entries, jax.random.fold_in(stream_key, 3), *heavy), -limit, limit).astype(held_as)


def setup_inputs(seed: int = 0) -> dict:
    key_list = jax.random.split(jax.random.key(seed), 10)
    block_input = noise_with(key_list[0], (TOKENS, MODEL_WIDTH), 1.0, 6.0, ((0, 8),), (0, 1, 8, 2.0))
    output_gradient = noise_with(key_list[1], (TOKENS, MODEL_WIDTH), 1.0, 6.0, ((0, 8),), (0, 1, 8, 2.0))
    queries = draw_queries(jax.random.fold_in(key_list[9], 71), 0)
    saved_keys = draw_saved_keys(jax.random.fold_in(key_list[9], 71), 0)
    values = scatter_about(key_list[4], (TOKENS, HEAD_COLUMNS), 1.0, 6.0, ((0, 8), (1, 4)))
    document_index = draw_document_index(jax.random.fold_in(key_list[9], 71), 0)
    output_weight = scatter_about(key_list[6], (MODEL_WIDTH, HEAD_COLUMNS), HEAD_COLUMNS ** -0.5, 0.109375, ((0, 8), (1, 4)))
    adapter_down_weight = scatter_about(key_list[7], (N_SECTION, MODEL_WIDTH, ADAPTER_RANK), MODEL_WIDTH ** -0.5, 0.078125, ((0, 2),))
    adapter_up_weight = scatter_about(key_list[8], (N_SECTION, ADAPTER_RANK, HEAD_COLUMNS), ADAPTER_RANK ** -0.5, 0.5, ((0, 2), (2, 4)))
    return {"block_input": block_input, "output_gradient": output_gradient, "queries": queries, "saved_keys": saved_keys, "values": values, "document_index": document_index, "output_weight": output_weight, "adapter_down_weight": adapter_down_weight, "adapter_up_weight": adapter_up_weight}


def attend(query_blk, key_blk, value_blk, grad_blk, doc_blk):
    token_rows = query_blk.shape[0]
    score_scale = HD ** -0.5
    query_heads = query_blk.reshape(token_rows, HEADS, HD).astype(jnp.float32)
    key_heads = key_blk.reshape(token_rows, HEADS, HD).astype(jnp.float32)
    value_heads = value_blk.reshape(token_rows, HEADS, HD).astype(jnp.float32)
    grad_heads = grad_blk.reshape(token_rows, HEADS, HD).astype(jnp.float32)
    scores = jnp.einsum("qhd,khd->hqk", query_heads, key_heads) * score_scale
    position = jnp.arange(token_rows, dtype=jnp.int32)
    allowed = (doc_blk[:, None] == doc_blk[None, :]) & (position[None, :] <= position[:, None])
    scores = jnp.where(allowed[None], scores, jnp.float32(-1e30))
    top_score = jnp.max(scores, axis=-1, keepdims=True)
    expo = jnp.exp(scores - top_score)
    attn_probs = expo / jnp.sum(expo, axis=-1, keepdims=True)
    probs_half = attn_probs.astype(jnp.bfloat16).astype(jnp.float32)
    output = jnp.einsum("hqk,khd->qhd", probs_half, value_heads).astype(jnp.bfloat16)
    value_gradient = jnp.einsum("hqk,qhd->khd", probs_half, grad_heads).astype(jnp.bfloat16)
    grad_prob = jnp.einsum("qhd,khd->hqk", grad_heads, value_heads)
    row_delta = jnp.sum(attn_probs * grad_prob, axis=-1, keepdims=True)
    grad_score = (attn_probs * (grad_prob - row_delta) * score_scale).astype(jnp.bfloat16).astype(jnp.float32)
    grad_query = jnp.einsum("hqk,khd->qhd", grad_score, key_heads).astype(jnp.bfloat16)
    grad_key = jnp.einsum("hqk,qhd->khd", grad_score, query_heads).astype(jnp.bfloat16)
    width = HEADS * HD
    return (output.reshape(token_rows, width), value_gradient.reshape(token_rows, width),
            grad_query.reshape(token_rows, width), grad_key.reshape(token_rows, width))


def rounded(term):
    half = lax.optimization_barrier(term.astype(jnp.bfloat16))
    return half.astype(jnp.float32)


def reference(block_input, output_gradient, queries, saved_keys, values, document_index, output_weight, adapter_down_weight, adapter_up_weight):
    width = HEADS * HD
    attn_grad = jnp.dot(output_gradient, output_weight, preferred_element_type=jnp.float32).astype(jnp.bfloat16)
    block_count = N_SECTION * N_DP

    def one_block(carry, index):
        sum_out, sum_value, summed_down_gradient, summed_up_gradient = carry
        start = (index * REPLICA_TOKENS).astype(jnp.int32)
        input_blk = lax.dynamic_slice_in_dim(block_input, start, REPLICA_TOKENS, 0)
        grad_blk = lax.dynamic_slice_in_dim(output_gradient, start, REPLICA_TOKENS, 0)
        output, value_gradient, grad_query, grad_key = attend(
            lax.dynamic_slice_in_dim(queries, start, REPLICA_TOKENS, 0),
            lax.dynamic_slice_in_dim(saved_keys, start, REPLICA_TOKENS, 0),
            lax.dynamic_slice_in_dim(values, start, REPLICA_TOKENS, 0),
            lax.dynamic_slice_in_dim(attn_grad, start, REPLICA_TOKENS, 0),
            lax.dynamic_slice_in_dim(document_index, start, REPLICA_TOKENS, 0))
        sum_out = sum_out + rounded(jnp.dot(grad_blk.T, output, preferred_element_type=jnp.float32))
        sum_value = sum_value + rounded(jnp.dot(input_blk.T, value_gradient, preferred_element_type=jnp.float32))
        invocation_index = (index // N_DP).astype(jnp.int32)
        down_matrix = lax.dynamic_index_in_dim(adapter_down_weight, invocation_index, 0, keepdims=False)
        up_matrix = lax.dynamic_index_in_dim(adapter_up_weight, invocation_index, 0, keepdims=False)
        narrow_product = jnp.dot(input_blk, down_matrix, preferred_element_type=jnp.float32).astype(jnp.bfloat16)
        mix_term = jnp.dot(value_gradient, up_matrix.T, preferred_element_type=jnp.float32).astype(jnp.bfloat16)
        down_term = jnp.dot(input_blk.T, mix_term, preferred_element_type=jnp.float32)
        up_term = jnp.dot(narrow_product.T, value_gradient, preferred_element_type=jnp.float32)
        summed_down_gradient = summed_down_gradient.at[invocation_index].add(down_term)
        summed_up_gradient = summed_up_gradient.at[invocation_index].add(up_term)
        return (sum_out, sum_value, summed_down_gradient, summed_up_gradient), (grad_query, grad_key)

    start_carry = (jnp.zeros((MODEL_WIDTH, width), jnp.float32), jnp.zeros((MODEL_WIDTH, width), jnp.float32),
                   jnp.zeros((N_SECTION, MODEL_WIDTH, ADAPTER_RANK), jnp.float32), jnp.zeros((N_SECTION, ADAPTER_RANK, width), jnp.float32))
    final, stacked = lax.scan(one_block, start_carry, jnp.arange(block_count, dtype=jnp.int32))
    sum_out, sum_value, summed_down_gradient, summed_up_gradient = final
    token_factor = TOKENS ** -0.5
    adapter_factor = (N_DP * REPLICA_TOKENS) ** -0.5
    grad_query = stacked[0].reshape(TOKENS, width)
    grad_key = stacked[1].reshape(TOKENS, width)
    return (sum_out * token_factor, sum_value * token_factor, grad_query, grad_key,
            summed_down_gradient * adapter_factor, summed_up_gradient * adapter_factor)
```

```python
import functools

import jax
import jax.numpy as jnp
from jax import lax
from jax.experimental import pallas as pl
from jax.experimental.pallas import tpu as pltpu
from jax.sharding import PartitionSpec as P

HD = 128
F32 = jnp.float32
BF16 = jnp.bfloat16
NT = (((1,), (1,)), ((), ()))
TN = (((0,), (0,)), ((), ()))


def dot(a, b, dims=(((1,), (0,)), ((), ()))):
    return lax.dot_general(a, b, dims, preferred_element_type=F32)


def probs_of(q, k, doc_col, doc_row):
    rows = q.shape[0]
    scores = dot(q, k, NT) * (HD ** -0.5)
    below = lax.broadcasted_iota(jnp.int32, (rows, rows), 0) >= lax.broadcasted_iota(
        jnp.int32, (rows, rows), 1
    )
    scores = jnp.where((doc_col == doc_row) & below, scores, F32(-1e30))
    expo = jnp.exp(scores - jnp.max(scores, axis=-1, keepdims=True))
    return expo / jnp.sum(expo, axis=-1, keepdims=True)


def output_kernel(q, k, v, doc_col, doc_row, out, half):
    probs = probs_of(q[...], k[...], doc_col[...], doc_row[...]).astype(BF16)
    half[0] = probs
    out[...] = dot(probs, v[...]).astype(BF16)


def value_kernel(half, g, out):
    out[...] = dot(half[0], g[...], TN).astype(BF16)


def score_kernel(q, k, v, g, doc_col, doc_row, grad_q, grad_k):
    probs = probs_of(q[...], k[...], doc_col[...], doc_row[...])
    grad_prob = dot(g[...], v[...], NT)
    row_delta = jnp.sum(probs * grad_prob, axis=-1, keepdims=True)
    grad_score = (probs * (grad_prob - row_delta) * (HD ** -0.5)).astype(BF16)
    grad_q[...] = dot(grad_score, k[...]).astype(BF16)
    grad_k[...] = dot(grad_score, q[...], TN).astype(BF16)


def attention_calls(rows, width):
    heads = width // HD
    head = pl.BlockSpec((rows, HD), lambda h: (0, h))
    col = pl.BlockSpec((rows, 1), lambda h: (0, 0))
    row = pl.BlockSpec((1, rows), lambda h: (0, 0))
    square = pl.BlockSpec((1, rows, rows), lambda h: (h, 0, 0))
    flat = jax.ShapeDtypeStruct((rows, width), BF16)
    params = pltpu.CompilerParams(vmem_limit_bytes=24 << 20)

    def call(kernel, in_specs, out_specs, out_shape, name, dots):
        return pl.pallas_call(
            kernel,
            grid=(heads,),
            in_specs=in_specs,
            out_specs=out_specs,
            out_shape=out_shape,
            compiler_params=params,
            name=name,
            cost_estimate=pl.CostEstimate(
                flops=dots * 2 * rows * rows * width,
                bytes_accessed=(len(in_specs) + 1) * rows * width * 2,
                transcendentals=heads * rows * rows,
            ),
        )

    forward = call(
        output_kernel,
        [head, head, head, col, row],
        (head, square),
        (flat, jax.ShapeDtypeStruct((heads, rows, rows), BF16)),
        "attend_out",
        2,
    )
    value = call(value_kernel, [square, head], head, flat, "value_grad", 1)
    scores = call(
        score_kernel,
        [head, head, head, head, col, row],
        (head, head),
        (flat, flat),
        "score_grads",
        4,
    )
    return forward, value, scores


def local(
    block_input,
    output_gradient,
    queries,
    saved_keys,
    values,
    document_index,
    output_weight,
    adapter_down_weight,
    adapter_up_weight,
):
    n_sec, n_dp, n_ten = (lax.axis_size(a) for a in ("section", "dp", "tensor"))
    sec, dp, ten = (lax.axis_index(a) for a in ("section", "dp", "tensor"))
    rows, width = block_input.shape
    local_width = queries.shape[1]
    part = width // n_sec
    piece = part // n_ten
    shard_rows = output_weight.shape[0]

    def shift(x, axis, by):
        size = lax.axis_size(axis)
        return lax.ppermute(x, axis, [(i, (i + by) % size) for i in range(size)])

    def columns(x, start, size):
        return lax.dynamic_slice_in_dim(x, start, size, 1)

    shards = []
    for k in range(n_dp):
        here = output_weight if k == 0 else shift(output_weight, "dp", k)
        shards.append((0, k, here))
        for j in range(1, n_sec):
            shards.append((j, k, shift(here, "section", j)))

    def regroup(x):
        gathered = [columns(x, sec * part, part)]
        for j in range(1, n_sec):
            sent = columns(x, ((sec + j) % n_sec) * part + ten * piece, piece)
            mine = shift(sent, "section", j)
            whole = jnp.zeros((rows, part), x.dtype)
            for m in range(n_ten):
                got = mine if m == 0 else shift(mine, "tensor", m)
                place = ((ten + n_ten - m) % n_ten) * piece
                whole = lax.dynamic_update_slice_in_dim(whole, got, place, 1)
            gathered.append(whole)
        return jnp.concatenate(gathered, axis=0)

    def across_sections(x):
        return jnp.concatenate([x] + [shift(x, "section", j) for j in range(1, n_sec)], axis=0)

    forward, value, scores = attention_calls(rows, local_width)
    doc_col, doc_row = document_index[:, None], document_index[None, :]
    output, probs_half = forward(queries, saved_keys, values, doc_col, doc_row)
    grad_rows = regroup(output_gradient)
    out_term = dot(grad_rows, across_sections(output), TN).astype(BF16)
    out_sum = lax.psum_scatter(out_term, "dp", scatter_dimension=0, tiled=True)

    attn_grad = jnp.zeros((rows, local_width), F32)
    for j, k, shard in shards:
        owner = ((sec + n_sec - j) % n_sec) * n_dp + (dp + n_dp - k) % n_dp
        attn_grad += dot(columns(output_gradient, owner * shard_rows, shard_rows), shard)
    attn_grad = attn_grad.astype(BF16)

    value_gradient = value(probs_half, attn_grad)
    value_term = dot(regroup(block_input), across_sections(value_gradient), TN).astype(BF16)
    value_sum = lax.psum_scatter(value_term, "dp", scatter_dimension=0, tiled=True)
    grad_query, grad_key = scores(
        queries, saved_keys, values, attn_grad, doc_col, doc_row
    )

    def sum_over_dp(blocks):
        take = functools.partial(lax.dynamic_index_in_dim, blocks, axis=0, keepdims=False)
        total = take(dp)
        for k in range(1, n_dp):
            total += shift(take((dp + k) % n_dp).astype(BF16), "dp", k).astype(F32)
        return total

    narrow = dot(block_input, adapter_down_weight[0]).astype(BF16)
    up_part = dot(narrow, value_gradient, TN)
    rank = up_part.shape[0]
    up_total = sum_over_dp(up_part.reshape(n_dp, rank // n_dp, local_width))

    mix = dot(value_gradient, adapter_up_weight[0], NT)
    mix_sent = mix.astype(BF16)
    for m in range(1, n_ten):
        mix += shift(mix_sent, "tensor", m).astype(F32)
    mix = mix.astype(BF16)
    out_rows = width // n_dp
    share = out_rows // n_ten
    strips = lax.dynamic_index_in_dim(
        block_input.reshape(rows, n_dp, n_ten, share), ten, 2, keepdims=False
    )
    down_part = dot(strips.reshape(rows, n_dp * share), mix, TN)
    down_mine = sum_over_dp(down_part.reshape(n_dp, share, rank))
    down_total = jnp.zeros((out_rows, rank), F32)
    for m in range(n_ten):
        got = down_mine if m == 0 else shift(down_mine, "tensor", m)
        place = ((ten + n_ten - m) % n_ten) * share
        down_total = lax.dynamic_update_slice_in_dim(down_total, got, place, 0)

    token_factor = (rows * n_sec * n_dp) ** (-0.5)
    adapter_factor = (rows * n_dp) ** (-0.5)
    return (
        out_sum.astype(F32) * token_factor,
        value_sum.astype(F32) * token_factor,
        grad_query,
        grad_key,
        (down_total * adapter_factor)[None],
        (up_total * adapter_factor)[None],
    )


def solution(mesh):
    return jax.shard_map(
        local,
        mesh=mesh,
        in_specs=(
            P(("section", "dp"), None),
            P(("section", "dp"), None),
            P(("section", "dp"), "tensor"),
            P(("section", "dp"), "tensor"),
            P(("section", "dp"), "tensor"),
            P(("section", "dp")),
            P(("section", "dp"), "tensor"),
            P("section", None, None),
            P("section", None, "tensor"),
        ),
        out_specs=(
            P(("section", "dp"), "tensor"),
            P(("section", "dp"), "tensor"),
            P(("section", "dp"), "tensor"),
            P(("section", "dp"), "tensor"),
            P("section", "dp", None),
            P("section", "dp", "tensor"),
        ),
        check_vma=False,
    )
```

```python
import functools

import jax
import jax.numpy as jnp
from jax import lax
from jax.experimental import pallas as pl
from jax.experimental.pallas import tpu as pltpu
from jax.sharding import PartitionSpec as P

HD = 128
F32 = jnp.float32
BF16 = jnp.bfloat16
NT = (((1,), (1,)), ((), ()))
TN = (((0,), (0,)), ((), ()))


def dot(a, b, dims=(((1,), (0,)), ((), ()))):
    return lax.dot_general(a, b, dims, preferred_element_type=F32)


def probs_of(q, k, doc_col, doc_row):
    rows = q.shape[0]
    scores = dot(q, k, NT) * (HD ** -0.5)
    below = lax.broadcasted_iota(jnp.int32, (rows, rows), 0) >= lax.broadcasted_iota(
        jnp.int32, (rows, rows), 1
    )
    scores = jnp.where((doc_col == doc_row) & below, scores, F32(-1e30))
    expo = jnp.exp(scores - jnp.max(scores, axis=-1, keepdims=True))
    return expo / jnp.sum(expo, axis=-1, keepdims=True)


def output_kernel(q, k, v, doc_col, doc_row, out, half):
    probs = probs_of(q[...], k[...], doc_col[...], doc_row[...]).astype(BF16)
    half[0] = probs
    out[...] = dot(probs, v[...]).astype(BF16)


def value_kernel(half, g, out):
    out[...] = dot(half[0], g[...], TN).astype(BF16)


def score_kernel(q, k, v, g, doc_col, doc_row, grad_q, grad_k):
    probs = probs_of(q[...], k[...], doc_col[...], doc_row[...])
    grad_prob = dot(g[...], v[...], NT)
    row_delta = jnp.sum(probs * grad_prob, axis=-1, keepdims=True)
    grad_score = (probs * (grad_prob - row_delta) * (HD ** -0.5)).astype(BF16)
    grad_q[...] = dot(grad_score, k[...]).astype(BF16)
    grad_k[...] = dot(grad_score, q[...], TN).astype(BF16)


def attention_calls(rows, width):
    heads = width // HD
    head = pl.BlockSpec((rows, HD), lambda h: (0, h))
    col = pl.BlockSpec((rows, 1), lambda h: (0, 0))
    row = pl.BlockSpec((1, rows), lambda h: (0, 0))
    square = pl.BlockSpec((1, rows, rows), lambda h: (h, 0, 0))
    flat = jax.ShapeDtypeStruct((rows, width), BF16)
    params = pltpu.CompilerParams(vmem_limit_bytes=24 << 20)

    def call(kernel, in_specs, out_specs, out_shape, name, dots):
        return pl.pallas_call(
            kernel,
            grid=(heads,),
            in_specs=in_specs,
            out_specs=out_specs,
            out_shape=out_shape,
            compiler_params=params,
            name=name,
            cost_estimate=pl.CostEstimate(
                flops=dots * 2 * rows * rows * width,
                bytes_accessed=(len(in_specs) + 1) * rows * width * 2,
                transcendentals=heads * rows * rows,
            ),
        )

    forward = call(
        output_kernel,
        [head, head, head, col, row],
        (head, square),
        (flat, jax.ShapeDtypeStruct((heads, rows, rows), BF16)),
        "attend_out",
        2,
    )
    value = call(value_kernel, [square, head], head, flat, "value_grad", 1)
    scores = call(
        score_kernel,
        [head, head, head, head, col, row],
        (head, head),
        (flat, flat),
        "score_grads",
        4,
    )
    return forward, value, scores


def local(
    block_input,
    output_gradient,
    queries,
    saved_keys,
    values,
    document_index,
    output_weight,
    adapter_down_weight,
    adapter_up_weight,
):
    n_sec, n_dp, n_ten = (lax.axis_size(a) for a in ("section", "dp", "tensor"))
    sec, dp, ten = (lax.axis_index(a) for a in ("section", "dp", "tensor"))
    rows, width = block_input.shape
    local_width = queries.shape[1]
    part = width // n_sec
    piece = part // n_ten
    shard_rows = output_weight.shape[0]

    def shift(x, axis, by):
        size = lax.axis_size(axis)
        return lax.ppermute(x, axis, [(i, (i + by) % size) for i in range(size)])

    def columns(x, start, size):
        return lax.dynamic_slice_in_dim(x, start, size, 1)

    def step(x, by):
        pairs = [(i, i + by) for i in range(n_dp) if 0 <= i + by < n_dp]
        return lax.ppermute(x, "dp", pairs)

    order = [
        sorted((d - o for o in range(n_dp) if o != d), key=lambda hop: (abs(hop), hop < 0))
        for d in range(n_dp)
    ]

    def pick(choices, values):
        out = values[choices[0]]
        for hop in sorted(set(choices) - {choices[0]}):
            held = functools.reduce(
                jnp.logical_or, [dp == d for d in range(n_dp) if choices[d] == hop]
            )
            out = jnp.where(held, values[hop], out)
        return out

    def forwards(x):
        return [shift(x, "section", j) for j in range(1, n_sec)]

    arrivals = {0: output_weight}
    slots = [(dp, output_weight, forwards(output_weight))]
    below, above = output_weight, output_weight
    for k in range(1, n_dp):
        below, above = step(below, 1), step(above, -1)
        arrivals[k], arrivals[-k] = below, above
        choices = [order[d][k - 1] for d in range(n_dp)]
        sent = slots[k - 2][2] if k > 1 else []
        here, below, above, sent = lax.optimization_barrier(
            (pick(choices, arrivals), below, above, sent)
        )
        if k > 1:
            slots[k - 2] = (*slots[k - 2][:2], sent)
        hops = {hop: jnp.int32(hop) for hop in arrivals}
        slots.append((dp - pick(choices, hops), here, forwards(here)))

    def regroup(x):
        gathered = [columns(x, sec * part, part)]
        for j in range(1, n_sec):
            sent = columns(x, ((sec + j) % n_sec) * part + ten * piece, piece)
            mine = shift(sent, "section", j)
            whole = jnp.zeros((rows, part), x.dtype)
            for m in range(n_ten):
                got = mine if m == 0 else shift(mine, "tensor", m)
                place = ((ten + n_ten - m) % n_ten) * piece
                whole = lax.dynamic_update_slice_in_dim(whole, got, place, 1)
            gathered.append(whole)
        return jnp.concatenate(gathered, axis=0)

    def across_sections(x):
        return jnp.concatenate([x] + [shift(x, "section", j) for j in range(1, n_sec)], axis=0)

    forward, value, scores = attention_calls(rows, local_width)
    doc_col, doc_row = document_index[:, None], document_index[None, :]
    output, probs_half = forward(queries, saved_keys, values, doc_col, doc_row)
    grad_rows = regroup(output_gradient)
    output_rows, kept = lax.optimization_barrier(
        (across_sections(output), [here for _, here, _ in slots])
    )
    out_term = dot(grad_rows, output_rows, TN).astype(BF16)
    out_sum = lax.psum_scatter(out_term, "dp", scatter_dimension=0, tiled=True)

    attn_grad = jnp.zeros((rows, local_width), F32)
    for (owner_dp, _, sent), here in zip(slots, kept):
        for j, shard in enumerate([here] + list(sent)):
            owner = ((sec + n_sec - j) % n_sec) * n_dp + owner_dp
            attn_grad += dot(columns(output_gradient, owner * shard_rows, shard_rows), shard)
    attn_grad = attn_grad.astype(BF16)

    value_gradient = value(probs_half, attn_grad)
    value_term = dot(regroup(block_input), across_sections(value_gradient), TN).astype(BF16)
    value_sum = lax.psum_scatter(value_term, "dp", scatter_dimension=0, tiled=True)
    grad_query, grad_key = scores(
        queries, saved_keys, values, attn_grad, doc_col, doc_row
    )

    def sum_over_dp(blocks):
        take = functools.partial(lax.dynamic_index_in_dim, blocks, axis=0, keepdims=False)
        total = take(dp)
        for k in range(1, n_dp):
            total += shift(take((dp + k) % n_dp).astype(BF16), "dp", k).astype(F32)
        return total

    narrow = dot(block_input, adapter_down_weight[0]).astype(BF16)
    up_part = dot(narrow, value_gradient, TN)
    rank = up_part.shape[0]
    up_total = sum_over_dp(up_part.reshape(n_dp, rank // n_dp, local_width))

    mix = dot(value_gradient, adapter_up_weight[0], NT)
    mix_sent = mix.astype(BF16)
    for m in range(1, n_ten):
        mix += shift(mix_sent, "tensor", m).astype(F32)
    mix = mix.astype(BF16)
    out_rows = width // n_dp
    share = out_rows // n_ten
    strips = jnp.concatenate(
        [columns(block_input, k * out_rows + ten * share, share) for k in range(n_dp)], axis=1
    )
    down_part = dot(strips, mix, TN)
    down_mine = sum_over_dp(down_part.reshape(n_dp, share, rank))
    down_total = jnp.zeros((out_rows, rank), F32)
    for m in range(n_ten):
        got = down_mine if m == 0 else shift(down_mine, "tensor", m)
        place = ((ten + n_ten - m) % n_ten) * share
        down_total = lax.dynamic_update_slice_in_dim(down_total, got, place, 0)

    token_factor = (rows * n_sec * n_dp) ** (-0.5)
    adapter_factor = (rows * n_dp) ** (-0.5)
    return (
        out_sum.astype(F32) * token_factor,
        value_sum.astype(F32) * token_factor,
        grad_query,
        grad_key,
        (down_total * adapter_factor)[None],
        (up_total * adapter_factor)[None],
    )


def solution(mesh):
    return jax.shard_map(
        local,
        mesh=mesh,
        in_specs=(
            P(("section", "dp"), None),
            P(("section", "dp"), None),
            P(("section", "dp"), "tensor"),
            P(("section", "dp"), "tensor"),
            P(("section", "dp"), "tensor"),
            P(("section", "dp")),
            P(("section", "dp"), "tensor"),
            P("section", None, None),
            P("section", None, "tensor"),
        ),
        out_specs=(
            P(("section", "dp"), "tensor"),
            P(("section", "dp"), "tensor"),
            P(("section", "dp"), "tensor"),
            P(("section", "dp"), "tensor"),
            P("section", "dp", None),
            P("section", "dp", "tensor"),
        ),
        check_vma=False,
    )
```

```python
import functools

import jax
import jax.numpy as jnp
from jax import lax
from jax.experimental import pallas as pl
from jax.experimental.pallas import tpu as pltpu
from jax.sharding import PartitionSpec as P

HD = 128
F32 = jnp.float32
BF16 = jnp.bfloat16
NT = (((1,), (1,)), ((), ()))
TN = (((0,), (0,)), ((), ()))


def dot(a, b, dims=(((1,), (0,)), ((), ()))):
    return lax.dot_general(a, b, dims, preferred_element_type=F32)


def probs_of(q, k, doc_col, doc_row):
    rows = q.shape[0]
    scores = dot(q, k, NT) * (HD ** -0.5)
    below = lax.broadcasted_iota(jnp.int32, (rows, rows), 0) >= lax.broadcasted_iota(
        jnp.int32, (rows, rows), 1
    )
    scores = jnp.where((doc_col == doc_row) & below, scores, F32(-1e30))
    expo = jnp.exp(scores - jnp.max(scores, axis=-1, keepdims=True))
    return expo / jnp.sum(expo, axis=-1, keepdims=True)


def output_kernel(q, k, v, doc_col, doc_row, out, half):
    probs = probs_of(q[...], k[...], doc_col[...], doc_row[...]).astype(BF16)
    half[0] = probs
    out[...] = dot(probs, v[...]).astype(BF16)


def value_kernel(half, g, out):
    out[...] = dot(half[0], g[...], TN).astype(BF16)


def score_kernel(q, k, v, g, doc_col, doc_row, grad_q, grad_k):
    probs = probs_of(q[...], k[...], doc_col[...], doc_row[...])
    grad_prob = dot(g[...], v[...], NT)
    row_delta = jnp.sum(probs * grad_prob, axis=-1, keepdims=True)
    grad_score = (probs * (grad_prob - row_delta) * (HD ** -0.5)).astype(BF16)
    grad_q[...] = dot(grad_score, k[...]).astype(BF16)
    grad_k[...] = dot(grad_score, q[...], TN).astype(BF16)


def attention_calls(rows, width):
    heads = width // HD
    head = pl.BlockSpec((rows, HD), lambda h: (0, h))
    col = pl.BlockSpec((rows, 1), lambda h: (0, 0))
    row = pl.BlockSpec((1, rows), lambda h: (0, 0))
    square = pl.BlockSpec((1, rows, rows), lambda h: (h, 0, 0))
    flat = jax.ShapeDtypeStruct((rows, width), BF16)
    params = pltpu.CompilerParams(vmem_limit_bytes=24 << 20)

    def call(kernel, in_specs, out_specs, out_shape, name, dots):
        return pl.pallas_call(
            kernel,
            grid=(heads,),
            in_specs=in_specs,
            out_specs=out_specs,
            out_shape=out_shape,
            compiler_params=params,
            name=name,
            cost_estimate=pl.CostEstimate(
                flops=dots * 2 * rows * rows * width,
                bytes_accessed=(len(in_specs) + 1) * rows * width * 2,
                transcendentals=heads * rows * rows,
            ),
        )

    forward = call(
        output_kernel,
        [head, head, head, col, row],
        (head, square),
        (flat, jax.ShapeDtypeStruct((heads, rows, rows), BF16)),
        "attend_out",
        2,
    )
    value = call(value_kernel, [square, head], head, flat, "value_grad", 1)
    scores = call(
        score_kernel,
        [head, head, head, head, col, row],
        (head, head),
        (flat, flat),
        "score_grads",
        4,
    )
    return forward, value, scores


def local(
    block_input,
    output_gradient,
    queries,
    saved_keys,
    values,
    document_index,
    output_weight,
    adapter_down_weight,
    adapter_up_weight,
):
    n_sec, n_dp, n_ten = (lax.axis_size(a) for a in ("section", "dp", "tensor"))
    sec, dp, ten = (lax.axis_index(a) for a in ("section", "dp", "tensor"))
    rows, width = block_input.shape
    local_width = queries.shape[1]
    part = width // n_sec
    piece = part // n_ten
    shard_rows = output_weight.shape[0]

    def shift(x, axis, by):
        size = lax.axis_size(axis)
        return lax.ppermute(x, axis, [(i, (i + by) % size) for i in range(size)])

    def columns(x, start, size):
        return lax.dynamic_slice_in_dim(x, start, size, 1)

    def step(x, by):
        pairs = [(i, i + by) for i in range(n_dp) if 0 <= i + by < n_dp]
        return lax.ppermute(x, "dp", pairs)

    order = [
        sorted((d - o for o in range(n_dp) if o != d), key=lambda hop: (abs(hop), hop < 0))
        for d in range(n_dp)
    ]

    def pick(choices, values):
        out = values[choices[0]]
        for hop in sorted(set(choices) - {choices[0]}):
            held = functools.reduce(
                jnp.logical_or, [dp == d for d in range(n_dp) if choices[d] == hop]
            )
            out = jnp.where(held, values[hop], out)
        return out

    def forwards(x):
        return [shift(x, "section", j) for j in range(1, n_sec)]

    arrivals = {0: output_weight}
    slots = [(dp, output_weight, forwards(output_weight))]
    below, above = output_weight, output_weight
    for k in range(1, n_dp):
        below, above = step(below, 1), step(above, -1)
        arrivals[k], arrivals[-k] = below, above
        choices = [order[d][k - 1] for d in range(n_dp)]
        sent = slots[k - 1][2]
        here, below, above, sent = lax.optimization_barrier(
            (pick(choices, arrivals), below, above, sent)
        )
        slots[k - 1] = (*slots[k - 1][:2], sent)
        hops = {hop: jnp.int32(hop) for hop in arrivals}
        slots.append((dp - pick(choices, hops), here, forwards(here)))

    def regroup(x):
        gathered = [columns(x, sec * part, part)]
        for j in range(1, n_sec):
            sent = columns(x, ((sec + j) % n_sec) * part + ten * piece, piece)
            mine = shift(sent, "section", j)
            whole = jnp.zeros((rows, part), x.dtype)
            for m in range(n_ten):
                got = mine if m == 0 else shift(mine, "tensor", m)
                place = ((ten + n_ten - m) % n_ten) * piece
                whole = lax.dynamic_update_slice_in_dim(whole, got, place, 1)
            gathered.append(whole)
        return jnp.concatenate(gathered, axis=0)

    def across_sections(x):
        return jnp.concatenate([x] + [shift(x, "section", j) for j in range(1, n_sec)], axis=0)

    forward, value, scores = attention_calls(rows, local_width)
    doc_col, doc_row = document_index[:, None], document_index[None, :]
    output, probs_half = forward(queries, saved_keys, values, doc_col, doc_row)
    grad_rows = regroup(output_gradient)
    output_rows, kept = lax.optimization_barrier(
        (across_sections(output), [here for _, here, _ in slots])
    )
    out_term = dot(grad_rows, output_rows, TN).astype(BF16)
    out_sum = lax.psum_scatter(out_term, "dp", scatter_dimension=0, tiled=True)

    attn_grad = jnp.zeros((rows, local_width), F32)
    for (owner_dp, _, sent), here in zip(slots, kept):
        for j, shard in enumerate([here] + list(sent)):
            owner = ((sec + n_sec - j) % n_sec) * n_dp + owner_dp
            attn_grad += dot(columns(output_gradient, owner * shard_rows, shard_rows), shard)
    attn_grad = attn_grad.astype(BF16)

    value_gradient = value(probs_half, attn_grad)
    value_term = dot(regroup(block_input), across_sections(value_gradient), TN).astype(BF16)
    value_sum = lax.psum_scatter(value_term, "dp", scatter_dimension=0, tiled=True)
    grad_query, grad_key = scores(
        queries, saved_keys, values, attn_grad, doc_col, doc_row
    )

    def sum_over_dp(blocks):
        take = functools.partial(lax.dynamic_index_in_dim, blocks, axis=0, keepdims=False)
        total = take(dp)
        for k in range(1, n_dp):
            total += shift(take((dp + k) % n_dp).astype(BF16), "dp", k).astype(F32)
        return total

    narrow = dot(block_input, adapter_down_weight[0]).astype(BF16)
    up_part = dot(narrow, value_gradient, TN)
    rank = up_part.shape[0]
    up_total = sum_over_dp(up_part.reshape(n_dp, rank // n_dp, local_width))

    mix = dot(value_gradient, adapter_up_weight[0], NT)
    mix_sent = mix.astype(BF16)
    for m in range(1, n_ten):
        mix += shift(mix_sent, "tensor", m).astype(F32)
    mix = mix.astype(BF16)
    out_rows = width // n_dp
    share = out_rows // n_ten
    strips = jnp.concatenate(
        [columns(block_input, k * out_rows + ten * share, share) for k in range(n_dp)], axis=1
    )
    down_part = dot(strips, mix, TN)
    down_mine = sum_over_dp(down_part.reshape(n_dp, share, rank))
    down_total = jnp.zeros((out_rows, rank), F32)
    for m in range(n_ten):
        got = down_mine if m == 0 else shift(down_mine, "tensor", m)
        place = ((ten + n_ten - m) % n_ten) * share
        down_total = lax.dynamic_update_slice_in_dim(down_total, got, place, 0)

    token_factor = (rows * n_sec * n_dp) ** (-0.5)
    adapter_factor = (rows * n_dp) ** (-0.5)
    return (
        out_sum.astype(F32) * token_factor,
        value_sum.astype(F32) * token_factor,
        grad_query,
        grad_key,
        (down_total * adapter_factor)[None],
        (up_total * adapter_factor)[None],
    )


def solution(mesh):
    return jax.shard_map(
        local,
        mesh=mesh,
        in_specs=(
            P(("section", "dp"), None),
            P(("section", "dp"), None),
            P(("section", "dp"), "tensor"),
            P(("section", "dp"), "tensor"),
            P(("section", "dp"), "tensor"),
            P(("section", "dp")),
            P(("section", "dp"), "tensor"),
            P("section", None, None),
            P("section", None, "tensor"),
        ),
        out_specs=(
            P(("section", "dp"), "tensor"),
            P(("section", "dp"), "tensor"),
            P(("section", "dp"), "tensor"),
            P(("section", "dp"), "tensor"),
            P("section", "dp", None),
            P("section", "dp", "tensor"),
        ),
        check_vma=False,
    )
```

```python
import functools

import jax
import jax.numpy as jnp
from jax import lax
from jax.experimental import pallas as pl
from jax.experimental.pallas import tpu as pltpu
from jax.sharding import PartitionSpec as P

HD = 128
F32 = jnp.float32
BF16 = jnp.bfloat16
NT = (((1,), (1,)), ((), ()))
TN = (((0,), (0,)), ((), ()))


def dot(a, b, dims=(((1,), (0,)), ((), ()))):
    return lax.dot_general(a, b, dims, preferred_element_type=F32)


def probs_of(q, k, doc_col, doc_row):
    rows = q.shape[0]
    scores = dot(q, k, NT) * (HD ** -0.5)
    below = lax.broadcasted_iota(jnp.int32, (rows, rows), 0) >= lax.broadcasted_iota(
        jnp.int32, (rows, rows), 1
    )
    scores = jnp.where((doc_col == doc_row) & below, scores, F32(-1e30))
    expo = jnp.exp(scores - jnp.max(scores, axis=-1, keepdims=True))
    return expo / jnp.sum(expo, axis=-1, keepdims=True)


def output_kernel(q, k, v, doc_col, doc_row, out, half):
    probs = probs_of(q[...], k[...], doc_col[...], doc_row[...]).astype(BF16)
    half[0] = probs
    out[...] = dot(probs, v[...]).astype(BF16)


def value_kernel(half, g, out):
    out[...] = dot(half[0], g[...], TN).astype(BF16)


def score_kernel(q, k, v, g, doc_col, doc_row, grad_q, grad_k):
    probs = probs_of(q[...], k[...], doc_col[...], doc_row[...])
    grad_prob = dot(g[...], v[...], NT)
    row_delta = jnp.sum(probs * grad_prob, axis=-1, keepdims=True)
    grad_score = (probs * (grad_prob - row_delta) * (HD ** -0.5)).astype(BF16)
    grad_q[...] = dot(grad_score, k[...]).astype(BF16)
    grad_k[...] = dot(grad_score, q[...], TN).astype(BF16)


def attention_calls(rows, width):
    heads = width // HD
    head = pl.BlockSpec((rows, HD), lambda h: (0, h))
    col = pl.BlockSpec((rows, 1), lambda h: (0, 0))
    row = pl.BlockSpec((1, rows), lambda h: (0, 0))
    square = pl.BlockSpec((1, rows, rows), lambda h: (h, 0, 0))
    flat = jax.ShapeDtypeStruct((rows, width), BF16)
    params = pltpu.CompilerParams(vmem_limit_bytes=24 << 20)

    def call(kernel, in_specs, out_specs, out_shape, name, dots):
        return pl.pallas_call(
            kernel,
            grid=(heads,),
            in_specs=in_specs,
            out_specs=out_specs,
            out_shape=out_shape,
            compiler_params=params,
            name=name,
            cost_estimate=pl.CostEstimate(
                flops=dots * 2 * rows * rows * width,
                bytes_accessed=(len(in_specs) + 1) * rows * width * 2,
                transcendentals=heads * rows * rows,
            ),
        )

    forward = call(
        output_kernel,
        [head, head, head, col, row],
        (head, square),
        (flat, jax.ShapeDtypeStruct((heads, rows, rows), BF16)),
        "attend_out",
        2,
    )
    value = call(value_kernel, [square, head], head, flat, "value_grad", 1)
    scores = call(
        score_kernel,
        [head, head, head, head, col, row],
        (head, head),
        (flat, flat),
        "score_grads",
        4,
    )
    return forward, value, scores


def local(
    block_input,
    output_gradient,
    queries,
    saved_keys,
    values,
    document_index,
    output_weight,
    adapter_down_weight,
    adapter_up_weight,
):
    n_sec, n_dp, n_ten = (lax.axis_size(a) for a in ("section", "dp", "tensor"))
    sec, dp, ten = (lax.axis_index(a) for a in ("section", "dp", "tensor"))
    rows, width = block_input.shape
    local_width = queries.shape[1]
    part = width // n_sec
    piece = part // n_ten
    shard_rows = output_weight.shape[0]

    def shift(x, axis, by):
        size = lax.axis_size(axis)
        return lax.ppermute(x, axis, [(i, (i + by) % size) for i in range(size)])

    def columns(x, start, size):
        return lax.dynamic_slice_in_dim(x, start, size, 1)

    def step(x, by):
        pairs = [(i, i + by) for i in range(n_dp) if 0 <= i + by < n_dp]
        return lax.ppermute(x, "dp", pairs)

    order = [
        sorted((d - o for o in range(n_dp) if o != d), key=lambda hop: (abs(hop), hop < 0))
        for d in range(n_dp)
    ]

    def pick(choices, values):
        out = values[choices[0]]
        for hop in sorted(set(choices) - {choices[0]}):
            held = functools.reduce(
                jnp.logical_or, [dp == d for d in range(n_dp) if choices[d] == hop]
            )
            out = jnp.where(held, values[hop], out)
        return out

    def forwards(x):
        return [shift(x, "section", j) for j in range(1, n_sec)]

    arrivals = {0: output_weight}
    slots = [(dp, output_weight, forwards(output_weight))]
    below, above = output_weight, output_weight
    for k in range(1, n_dp):
        below, above = step(below, 1), step(above, -1)
        arrivals[k], arrivals[-k] = below, above
        choices = [order[d][k - 1] for d in range(n_dp)]
        sent = slots[k - 1][2]
        here, below, above, sent = lax.optimization_barrier(
            (pick(choices, arrivals), below, above, sent)
        )
        slots[k - 1] = (*slots[k - 1][:2], sent)
        hops = {hop: jnp.int32(hop) for hop in arrivals}
        slots.append((dp - pick(choices, hops), here, forwards(here)))

    def regroup(x, beside):
        gathered = [columns(x, sec * part, part)]
        for j in range(1, n_sec):
            sent = columns(x, ((sec + j) % n_sec) * part + ten * piece, piece)
            mine, beside = lax.optimization_barrier((shift(sent, "section", j), beside))
            whole = jnp.zeros((rows, part), x.dtype)
            for m in range(n_ten):
                got = mine if m == 0 else shift(mine, "tensor", m)
                place = ((ten + n_ten - m) % n_ten) * piece
                whole = lax.dynamic_update_slice_in_dim(whole, got, place, 1)
            gathered.append(whole)
        return jnp.concatenate(gathered, axis=0), beside

    def across_sections(x):
        return jnp.concatenate([x] + [shift(x, "section", j) for j in range(1, n_sec)], axis=0)

    forward, value, scores = attention_calls(rows, local_width)
    doc_col, doc_row = document_index[:, None], document_index[None, :]
    output, probs_half = forward(queries, saved_keys, values, doc_col, doc_row)
    grad_rows, _ = regroup(output_gradient, [])
    output_rows, kept = lax.optimization_barrier(
        (across_sections(output), [here for _, here, _ in slots])
    )
    out_term = dot(grad_rows, output_rows, TN).astype(BF16)
    out_sum = lax.psum_scatter(out_term, "dp", scatter_dimension=0, tiled=True)

    input_rows, last = regroup(block_input, slots[-1][2])
    slots[-1] = (*slots[-1][:2], last)
    attn_grad = jnp.zeros((rows, local_width), F32)
    for (owner_dp, _, sent), here in zip(slots, kept):
        for j, shard in enumerate([here] + list(sent)):
            owner = ((sec + n_sec - j) % n_sec) * n_dp + owner_dp
            attn_grad += dot(columns(output_gradient, owner * shard_rows, shard_rows), shard)
    attn_grad = attn_grad.astype(BF16)

    value_gradient = value(probs_half, attn_grad)
    value_term = dot(input_rows, across_sections(value_gradient), TN).astype(BF16)
    value_sum = lax.psum_scatter(value_term, "dp", scatter_dimension=0, tiled=True)
    grad_query, grad_key = scores(
        queries, saved_keys, values, attn_grad, doc_col, doc_row
    )

    def sum_over_dp(blocks):
        take = functools.partial(lax.dynamic_index_in_dim, blocks, axis=0, keepdims=False)
        total = take(dp)
        for k in range(1, n_dp):
            total += shift(take((dp + k) % n_dp).astype(BF16), "dp", k).astype(F32)
        return total

    narrow = dot(block_input, adapter_down_weight[0]).astype(BF16)
    up_part = dot(narrow, value_gradient, TN)
    rank = up_part.shape[0]
    up_total = sum_over_dp(up_part.reshape(n_dp, rank // n_dp, local_width))

    mix = dot(value_gradient, adapter_up_weight[0], NT)
    mix_sent = mix.astype(BF16)
    for m in range(1, n_ten):
        mix += shift(mix_sent, "tensor", m).astype(F32)
    mix = mix.astype(BF16)
    out_rows = width // n_dp
    share = out_rows // n_ten
    strips = jnp.concatenate(
        [columns(block_input, k * out_rows + ten * share, share) for k in range(n_dp)], axis=1
    )
    down_part = dot(strips, mix, TN)
    down_mine = sum_over_dp(down_part.reshape(n_dp, share, rank))
    down_total = jnp.zeros((out_rows, rank), F32)
    for m in range(n_ten):
        got = down_mine if m == 0 else shift(down_mine, "tensor", m)
        place = ((ten + n_ten - m) % n_ten) * share
        down_total = lax.dynamic_update_slice_in_dim(down_total, got, place, 0)

    token_factor = (rows * n_sec * n_dp) ** (-0.5)
    adapter_factor = (rows * n_dp) ** (-0.5)
    return (
        out_sum.astype(F32) * token_factor,
        value_sum.astype(F32) * token_factor,
        grad_query,
        grad_key,
        (down_total * adapter_factor)[None],
        (up_total * adapter_factor)[None],
    )


def solution(mesh):
    return jax.shard_map(
        local,
        mesh=mesh,
        in_specs=(
            P(("section", "dp"), None),
            P(("section", "dp"), None),
            P(("section", "dp"), "tensor"),
            P(("section", "dp"), "tensor"),
            P(("section", "dp"), "tensor"),
            P(("section", "dp")),
            P(("section", "dp"), "tensor"),
            P("section", None, None),
            P("section", None, "tensor"),
        ),
        out_specs=(
            P(("section", "dp"), "tensor"),
            P(("section", "dp"), "tensor"),
            P(("section", "dp"), "tensor"),
            P(("section", "dp"), "tensor"),
            P("section", "dp", None),
            P("section", "dp", "tensor"),
        ),
        check_vma=False,
    )
```
